32 devices in a mesh: rep: 8 (over y, x, core), tp: 4 (over z).
Axes of the slice: x: 2, y: 2, z: 4, core: 2. Of those that a mesh axis runs over, the one named last changes fastest.
Arguments:
- context: bfloat16 [16384, 5120], P('rep', 'tp'), may hold values from -6 to 6
- out_grad: bfloat16 [16384, 5120], P('rep', 'tp'), may hold values from -6 to 6
- rewards: int32 [8, 32], P(None, 'rep'), may hold values from 0 to 1
- master: float32 [5120, 5120], P('rep', 'tp'), may hold values from -0.078125 to 0.078125
- first_moment: float32 [5120, 5120], P('rep', 'tp'), may hold values from -0.046875 to 0.046875
- second_moment: float32 [5120, 5120], P('rep', 'tp'), may hold values from 6.1035155e-07 to 6.1035156e-05
- inputs: bfloat16 [4, 256, 5120], P(None, 'rep'), may hold values from -6 to 6
- w_query: bfloat16 [5120, 5120], P(None, 'tp'), may hold values from -0.078125 to 0.078125
- w_key: bfloat16 [5120, 1024], P(None, 'tp'), may hold values from -0.078125 to 0.078125
- w_value: bfloat16 [5120, 1024], P(None, 'tp'), may hold values from -0.078125 to 0.078125
- cache_keys: bfloat16 [256, 256, 1024], P('rep', None, 'tp'), may hold values from -400 to 400
- cache_values: bfloat16 [256, 256, 1024], P('rep', None, 'tp'), may hold values from -24 to 24
- lengths: int32 [32], P('rep'), may hold values from 64 to 256
Outputs:
- decoded: bfloat16 [4, 256, 5120], P(None, 'rep')
- adam_step: float32 [5120, 5120], P('rep', 'tp')
The draws below stay inside these ranges and needn't reach their ends.
All inputs are finite; a program needn't handle non-finite values.
Results may differ from the reference program's by a relative error of at most 0.0088.
Values may be sent and summed in bfloat16 or wider, within the bound.
No kernel may reach another device: no remote copies, remote signals or barrier semaphores. Data moves between devices by JAX's collectives and lax.ppermute only.
A program may use at most 192 MiB of HBM per device.

```python
import math
import jax
import jax.numpy as jnp
from jax import lax

D = 5120
HEADS = 40
KV_HEADS = 8
HEAD_DIM = 128
PROMPTS_L = 8
GROUP_DEV = 4
RESP_LEN = 64
CACHE = 256
ROLL_SAMP = 8
STEPS = 4
GROUP = 32
TOK_DEV = 2048
TOKENS = 16384
SEQS = 256
RPROMPTS = 32
N_REP = 8


def draw_rewards(key, part):
    sample_index = jnp.arange(GROUP, dtype=jnp.int32)[None, :]
    threshold = 150 + 700 * sample_index // (GROUP - 1)
    ticket = jax.random.randint(jax.random.fold_in(key, 21), (PROMPTS_L, GROUP), 0, 1000)
    return (ticket < threshold).astype(jnp.int32)


def draw_cache_keys(key, part):
    base = jax.random.normal(jax.random.fold_in(key, 11), (SEQS, CACHE, KV_HEADS * HEAD_DIM), jnp.float32)
    base = jnp.clip(base, -6.0, 6.0)
    return base.astype(jnp.bfloat16)


def set_ends(array, key, smallest, largest):
    longest = array.shape.index(max(array.shape))
    spots = []
    for shift in (0, 1):
        where = [jax.random.randint(jax.random.fold_in(key, axis), (), 0, length) for axis, length in enumerate(array.shape)]
        where[longest] = (where[longest] + shift) % array.shape[longest]
        spots.append(tuple(where))
    return array.at[spots[0]].set(smallest).at[spots[1]].set(largest)


def with_spikes(drawn, stream_key, source, target, shards_of, factor):
    def block_of(dim):
        return (jnp.arange(drawn.shape[dim]) // (drawn.shape[dim] // shards_of)).reshape((-1,) + (1,) * (drawn.ndim - 1 - dim))

    near = jax.random.permutation(stream_key, shards_of)[block_of(target)]
    far = (block_of(target) + shards_of // 2) % shards_of
    return jnp.where((block_of(source) == near) | (block_of(source) == far), factor * drawn, drawn)


def levels(key, dims, shards, least, top_value):
    factor_of = 1.0
    for position, shards_of in shards:
        steps = jax.random.uniform(jax.random.fold_in(jax.random.fold_in(key, 6), position), (shards_of,), jnp.float32, least / len(shards), top_value / len(shards))
        factor_of = factor_of * jnp.repeat(jnp.exp(steps), dims[position] // shards_of).reshape((-1,) + (1,) * (len(dims) - 1 - position))
    return factor_of


def noise(stream_key, shape, width, bound, cuts=(), kind=jnp.bfloat16):
    drawn = jax.random.normal(stream_key, shape, jnp.float32) * width
    if len(cuts) > 0:
        drawn = levels(stream_key, shape, cuts, -0.22, 0.18) * drawn
    return jnp.clip(drawn, min=-bound, max=bound).astype(kind)


def bell_draw_with(key, shape, spread, bound, pieces, heavy, held_as=jnp.bfloat16):
    result = spread * jax.random.normal(key, shape, jnp.float32)
    if pieces:
        result = result * levels(key, shape, pieces, -0.22, 0.18)
    return jnp.clip(with_spikes(result, jax.random.fold_in(key, 3), *heavy), -bound, bound).astype(held_as)


def setup_inputs(seed: int = 0) -> dict:
    key_list = jax.random.split(jax.random.key(seed), 14)
    return {
        "context": bell_draw_with(key_list[0], (TOKENS, HEADS * HEAD_DIM), 1.0, 6.0, ((0, 8), (1, 4)), (0, 1, 8, 2.0)),
        "out_grad": noise(key_list[1], (TOKENS, D), 1.0, 6.0, ((0, 8), (1, 4))),
        "rewards": draw_rewards(jax.random.fold_in(key_list[13], 71), 0),
        "master": noise(key_list[3], (HEADS * HEAD_DIM, D), (HEADS * HEAD_DIM) ** -0.5, 0.078125, ((0, 8), (1, 4)), jnp.float32),
        "first_moment": noise(key_list[4], (HEADS * HEAD_DIM, D), (0.4 * (TOK_DEV * N_REP) ** -0.5), 0.046875, ((0, 8), (1, 4)), jnp.float32),
        "second_moment": jnp.clip(jnp.exp(math.log(6.103515625e-05) - 4.6051702 * jax.random.uniform(key_list[5], (HEADS * HEAD_DIM, D), jnp.float32) ** levels(key_list[5], (HEADS * HEAD_DIM, D), ((0, 8), (1, 4)), -0.2, 0.2)), 6.103515488575795e-07, 6.103515625e-05),
        "inputs": noise(key_list[6], (STEPS, SEQS, D), 1.0, 6.0, ((1, 8),)),
        "w_query": noise(key_list[7], (D, HEADS * HEAD_DIM), D ** -0.5, 0.078125, ((1, 4),)),
        "w_key": noise(key_list[8], (D, KV_HEADS * HEAD_DIM), D ** -0.5, 0.078125, ((1, 4),)),
        "w_value": noise(key_list[9], (D, KV_HEADS * HEAD_DIM), D ** -0.5, 0.078125, ((1, 4),)),
        "cache_keys": draw_cache_keys(jax.random.fold_in(key_list[13], 71), 0),
        "cache_values": noise(key_list[11], (SEQS, CACHE, KV_HEADS * HEAD_DIM), 4.0, 24.0, ((0, 8), (2, 4))),
        "lengths": set_ends(jax.random.randint(key_list[12], (RPROMPTS,), CACHE // 4, CACHE + 1), jax.random.fold_in(key_list[12], 1), CACHE // 4, CACHE).astype(jnp.int32),
    }


rope_base = 1000000.0
first_beta = 0.9
second_beta = 0.95
adam_epsilon = 1e-08
step_count = 10
learn_rate = 0.001

def rotate(vectors, positions):
    half_dim = vectors.shape[-1] // 2
    frequency = rope_base ** (-2.0 * jnp.arange(half_dim, dtype=jnp.float32) / vectors.shape[-1])
    angles = positions[..., None].astype(jnp.float32) * frequency
    cosine_table = jnp.cos(angles)
    sine_table = jnp.sin(angles)
    former = vectors[..., :half_dim]
    latter = vectors[..., half_dim:]
    return jnp.concatenate([former * cosine_table - latter * sine_table, latter * cosine_table + former * sine_table], axis=-1)

def attend(queries, old_keys, old_values, new_keys, new_values, live_mask):
    score_scale = HEAD_DIM ** (-0.5)
    step_total = queries.shape[0]
    query_wide = queries.astype(jnp.float32)
    cache_scores = jnp.einsum('tsgqd,scgd->tsgqc', query_wide, old_keys.astype(jnp.float32)) * score_scale
    cache_scores = jnp.where(live_mask[None, :, None, None, :], cache_scores, -1e+30)
    recent = jnp.einsum('tsgqd,usgd->tsgqu', query_wide, new_keys.astype(jnp.float32)) * score_scale
    causal = jnp.arange(step_total)[:, None] >= jnp.arange(step_total)[None, :]
    recent = jnp.where(causal[:, None, None, None, :], recent, -1e+30)
    row_peak = jnp.maximum(lax.optimization_barrier(jnp.max(cache_scores, axis=-1)), lax.optimization_barrier(jnp.max(recent, axis=-1)))[..., None]
    cache_exp = jnp.exp(cache_scores - row_peak)
    recent_exp = jnp.exp(recent - row_peak)
    denominator = lax.optimization_barrier(jnp.sum(cache_exp, axis=-1, keepdims=True)) + lax.optimization_barrier(jnp.sum(recent_exp, axis=-1, keepdims=True))
    cache_weight = (cache_exp / denominator).astype(jnp.bfloat16)
    recent_weight = (recent_exp / denominator).astype(jnp.bfloat16)
    attended = jnp.einsum('tsgqc,scgd->tsgqd', cache_weight.astype(jnp.float32), old_values.astype(jnp.float32))
    attended = attended + jnp.einsum('tsgqu,usgd->tsgqd', recent_weight.astype(jnp.float32), new_values.astype(jnp.float32))
    return attended.astype(jnp.bfloat16)

def reference(context, out_grad, rewards, master, first_moment, second_moment, inputs, w_query, w_key, w_value, cache_keys, cache_values, lengths):
    group_size = rewards.shape[1]
    token_count = context.shape[0]
    totals = lax.optimization_barrier(jnp.sum(rewards.astype(jnp.float32), axis=1))
    advantage = rewards.astype(jnp.float32) - totals[:, None] / group_size
    ordered = advantage.reshape(PROMPTS_L, N_REP, GROUP_DEV).transpose(1, 0, 2).reshape(-1)
    per_token = jnp.repeat(ordered, RESP_LEN) / token_count
    scaled = (out_grad.astype(jnp.float32) * per_token[:, None]).astype(jnp.bfloat16)
    gradient = lax.dot_general(context, scaled, (((0,), (0,)), ((), ())), preferred_element_type=jnp.float32)
    moment_new = first_beta * first_moment + (1.0 - first_beta) * gradient
    square_new = second_beta * second_moment + (1.0 - second_beta) * gradient * gradient
    adam_step = moment_new / (1.0 - first_beta ** step_count) / (jnp.sqrt(square_new / (1.0 - second_beta ** step_count)) + adam_epsilon)
    weight = (master - learn_rate * adam_step).astype(jnp.bfloat16)
    step_total, seq_total, model_width = inputs.shape
    flat_rows = inputs.reshape(step_total * seq_total, model_width)
    queries = jnp.dot(flat_rows, w_query, preferred_element_type=jnp.float32).reshape(step_total, seq_total, HEADS, HEAD_DIM)
    key_new = jnp.dot(flat_rows, w_key, preferred_element_type=jnp.float32).reshape(step_total, seq_total, KV_HEADS, HEAD_DIM)
    value_new = jnp.dot(flat_rows, w_value, preferred_element_type=jnp.float32).reshape(step_total, seq_total, KV_HEADS, HEAD_DIM).astype(jnp.bfloat16)
    seq_length = jnp.repeat(lengths, ROLL_SAMP)
    positions = seq_length[None, :] + jnp.arange(step_total, dtype=jnp.int32)[:, None]
    queries = rotate(queries, positions[:, :, None]).astype(jnp.bfloat16)
    queries = queries.reshape(step_total, seq_total, KV_HEADS, HEADS // KV_HEADS, HEAD_DIM)
    key_new = rotate(key_new, positions[:, :, None]).astype(jnp.bfloat16)
    old_keys = cache_keys.reshape(seq_total, CACHE, KV_HEADS, HEAD_DIM)
    old_values = cache_values.reshape(seq_total, CACHE, KV_HEADS, HEAD_DIM)
    live_mask = jnp.arange(CACHE, dtype=jnp.int32)[None, :] < seq_length[:, None]
    attended = attend(queries, old_keys, old_values, key_new, value_new, live_mask)
    attended = attended.reshape(step_total * seq_total, HEADS * HEAD_DIM)
    decoded = jnp.dot(attended, weight, preferred_element_type=jnp.float32).astype(jnp.bfloat16)
    return (decoded.reshape(step_total, seq_total, model_width), adam_step)
```

```python
import jax
import jax.numpy as jnp
from jax import lax
from jax.sharding import PartitionSpec as P

HEAD_DIM = 128


rope_base = 1000000.0
first_beta = 0.9
second_beta = 0.95
adam_epsilon = 1e-08
step_count = 10
learn_rate = 0.001


bf16 = jnp.bfloat16
f32 = jnp.float32
AXES = ("rep", "tp")


def rotate(vectors, positions):
    half_dim = vectors.shape[-1] // 2
    frequency = rope_base ** (-2.0 * jnp.arange(half_dim, dtype=jnp.float32) / vectors.shape[-1])
    angles = positions[..., None].astype(jnp.float32) * frequency
    cosine_table = jnp.cos(angles)
    sine_table = jnp.sin(angles)
    former = vectors[..., :half_dim]
    latter = vectors[..., half_dim:]
    return jnp.concatenate(
        [former * cosine_table - latter * sine_table, latter * cosine_table + former * sine_table],
        axis=-1,
    )


def attend(queries, old_keys, old_values, new_keys, new_values, live_mask):
    score_scale = HEAD_DIM ** (-0.5)
    step_total = queries.shape[0]
    cache_scores = (
        jnp.einsum("tsgqd,scgd->tsgqc", queries, old_keys, preferred_element_type=jnp.float32)
        * score_scale
    )
    cache_scores = jnp.where(live_mask[None, :, None, None, :], cache_scores, -1e30)
    recent = (
        jnp.einsum("tsgqd,usgd->tsgqu", queries, new_keys, preferred_element_type=jnp.float32)
        * score_scale
    )
    causal = jnp.arange(step_total)[:, None] >= jnp.arange(step_total)[None, :]
    recent = jnp.where(causal[:, None, None, None, :], recent, -1e30)
    row_peak = jnp.maximum(jnp.max(cache_scores, axis=-1), jnp.max(recent, axis=-1))[..., None]
    cache_exp = jnp.exp(cache_scores - row_peak)
    recent_exp = jnp.exp(recent - row_peak)
    denominator = jnp.sum(cache_exp, axis=-1, keepdims=True) + jnp.sum(
        recent_exp, axis=-1, keepdims=True
    )
    cache_weight = (cache_exp / denominator).astype(jnp.bfloat16)
    recent_weight = (recent_exp / denominator).astype(jnp.bfloat16)
    attended = jnp.einsum(
        "tsgqc,scgd->tsgqd", cache_weight, old_values, preferred_element_type=jnp.float32
    )
    attended = attended + jnp.einsum(
        "tsgqu,usgd->tsgqd", recent_weight, new_values, preferred_element_type=jnp.float32
    )
    return attended.astype(jnp.bfloat16)


def decode_heads(inputs, w_query, w_key, w_value, cache_keys, cache_values, lengths):
    step_total, seq_local, model_width = inputs.shape
    local_heads = w_query.shape[1] // HEAD_DIM
    local_kv = w_key.shape[1] // HEAD_DIM
    flat_rows = inputs.reshape(step_total * seq_local, model_width)
    queries = jnp.dot(flat_rows, w_query, preferred_element_type=jnp.float32).reshape(
        step_total, seq_local, local_heads, HEAD_DIM
    )
    key_new = jnp.dot(flat_rows, w_key, preferred_element_type=jnp.float32).reshape(
        step_total, seq_local, local_kv, HEAD_DIM
    )
    value_new = (
        jnp.dot(flat_rows, w_value, preferred_element_type=jnp.float32)
        .reshape(step_total, seq_local, local_kv, HEAD_DIM)
        .astype(jnp.bfloat16)
    )
    seq_length = jnp.repeat(lengths, seq_local // lengths.shape[0])
    positions = seq_length[None, :] + jnp.arange(step_total, dtype=jnp.int32)[:, None]
    queries = rotate(queries, positions[:, :, None]).astype(jnp.bfloat16)
    queries = queries.reshape(step_total, seq_local, local_kv, local_heads // local_kv, HEAD_DIM)
    key_new = rotate(key_new, positions[:, :, None]).astype(jnp.bfloat16)
    slot_total = cache_keys.shape[1]
    old_keys = cache_keys.reshape(seq_local, slot_total, local_kv, HEAD_DIM)
    old_values = cache_values.reshape(seq_local, slot_total, local_kv, HEAD_DIM)
    live_mask = jnp.arange(slot_total, dtype=jnp.int32)[None, :] < seq_length[:, None]
    attended = attend(queries, old_keys, old_values, key_new, value_new, live_mask)
    return attended.reshape(step_total * seq_local, local_heads * HEAD_DIM)


def token_scale(context, rewards):
    replicas = lax.axis_size("rep")
    prompt_count, local_group = rewards.shape
    totals = lax.psum(jnp.sum(rewards, axis=1), "rep")
    group_size = local_group * replicas
    advantage = rewards.astype(jnp.float32) - totals.astype(jnp.float32)[:, None] / group_size
    token_local = context.shape[0]
    return jnp.repeat(advantage.reshape(-1), token_local // (prompt_count * local_group)) / (
        token_local * replicas
    )


def adam(gradient, first_moment, second_moment):
    moment_new = first_beta * first_moment + (1.0 - first_beta) * gradient
    square_new = second_beta * second_moment + (1.0 - second_beta) * gradient * gradient
    return (
        moment_new
        / (1.0 - first_beta**step_count)
        / (jnp.sqrt(square_new / (1.0 - second_beta**step_count)) + adam_epsilon)
    )


def outer_sum(rows, columns):
    return lax.dot_general(
        rows, columns, (((0,), (0,)), ((), ())), preferred_element_type=jnp.float32
    )


def bits_below(count):
    found = []
    bit = 1
    while bit < count:
        found.append(bit)
        bit *= 2
    return found


def pick(array, index):
    return lax.dynamic_index_in_dim(array, index, 0, keepdims=False)


class Layout:
    def __init__(self, replicas, planes):
        self.replicas = replicas
        self.planes = planes
        self.split = replicas // planes
        self.group_bits = bits_below(planes)
        self.split_bits = bits_below(self.split)
        self.strides = range(1, planes // 2)

    def hub(self, pair):
        return 2 * pair + 1 if pair < self.planes // 4 or self.planes == 2 else 2 * pair

    def outer(self, pair):
        return self.hub(pair) ^ 1

    def is_hub(self, plane):
        return self.hub(plane // 2) == plane

    def source(self, plane, kind):
        if kind == "own":
            return plane
        if not self.is_hub(plane):
            return None
        name, stride = kind
        pair = (plane // 2) ^ stride
        return self.hub(pair) if name == "hub" else self.outer(pair)

    def table(self, values):
        return pick(jnp.array(values), lax.axis_index("tp"))

    def send(self, array, target):
        moves = []
        for rep in range(self.replicas):
            for plane in range(self.planes):
                to = target(rep // self.split, rep % self.split, plane)
                if to is not None:
                    group, part, other = to
                    moves.append(
                        (
                            rep * self.planes + plane,
                            (group * self.split + part) * self.planes + other,
                        )
                    )
        return lax.ppermute(array, AXES, moves)

    def group(self):
        return lax.axis_index("rep") // self.split

    def part(self):
        return lax.axis_index("rep") % self.split

    def sum_parts(self, block):
        part = self.part()
        for bit in reversed(self.split_bits):
            mine = (part // bit) % 2
            halves = block.reshape((2, bit) + block.shape[1:])
            got = self.send(
                pick(halves, 1 - mine).astype(bf16),
                lambda g, u, z, bit=bit: (g, u ^ bit, z),
            )
            block = pick(halves, mine) + got.astype(f32)
        return block[0]

    def sum_to_owner(self, block, kind, bits):
        for bit in bits:

            def toward(g, u, z, bit=bit):
                owner = self.source(z, kind)
                if owner is None or (g ^ owner) & bit == 0:
                    return None
                return (g ^ bit, u, z)

            block = block + self.send(block.astype(bf16), toward).astype(f32)
        return block

    def reduce_pair(self, own, other, kind, first_bit):
        own = self.sum_parts(own)
        other = self.sum_parts(other)
        group = self.group()
        owner = self.table([self.source(z, kind) or 0 for z in range(self.planes)])
        near = (group ^ owner) & first_bit == 0

        def across(g, u, z):
            return None if self.source(z, kind) is None else (g ^ first_bit, u, z)

        got = self.send(jnp.where(near, other, own).astype(bf16), across)
        block = jnp.where(near, own, other) + got.astype(f32)

        def rest(g, u, z, bit):
            target = self.source(z, kind)
            if target is None or (g ^ target) & bit == 0:
                return None
            return (g ^ bit, u, z)

        for bit in self.group_bits:
            if bit != first_bit:
                block = block + self.send(
                    block.astype(bf16), lambda g, u, z, bit=bit: rest(g, u, z, bit)
                ).astype(f32)

        def onward(g, u, z):
            target = self.source(z, kind)
            if target is None or g != target ^ first_bit:
                return None
            return (target, u, z ^ 1)

        return block, self.send(block.astype(bf16), onward)

    def reduce_own_other(self, block):
        block = self.sum_parts(block)
        group = self.group()
        for bit in self.group_bits:
            mine = (group // bit) % 2
            halves = block.reshape((2, block.shape[0] // 2) + block.shape[1:])
            got = self.send(
                pick(halves, 1 - mine).astype(bf16),
                lambda g, u, z, bit=bit: (g ^ bit, u, z),
            )
            block = pick(halves, mine) + got.astype(f32)
        block = self.send(block.astype(bf16), lambda g, u, z: (g, u, z ^ 1))
        for bit in reversed(self.group_bits):

            def toward(g, u, z, bit=bit):
                return None if (g ^ z ^ 1) & bit == 0 else (g ^ bit, u, z)

            got = self.send(block, toward)
            low = (group // bit) % 2 == 0
            block = jnp.where(
                low,
                jnp.concatenate([block, got], axis=0),
                jnp.concatenate([got, block], axis=0),
            )
        return block

    def gather_planes(self, block, axis):
        plane = lax.axis_index("tp")
        width = block.shape[axis]
        found = [(plane, block)]
        partner = self.send(block, lambda g, u, z: (g, u, z ^ 1))
        found.append((plane ^ 1, partner))
        hub_here = self.table([self.is_hub(z) for z in range(self.planes)])
        for stride in self.strides:

            def hop(g, u, z, stride=stride):
                return (g, u, self.hub((z // 2) ^ stride)) if self.is_hub(z) else None

            def out(g, u, z):
                return (g, u, z ^ 1) if self.is_hub(z) else None

            for kind, source in ((("hub", stride), block), (("outer", stride), partner)):
                got = self.send(source, hop)
                passed = self.send(got, out)
                order = []
                for z in range(self.planes):
                    order.append(self.source(self.hub(z // 2), kind))
                found.append((self.table(order), jnp.where(hub_here, got, passed)))
        shape = list(block.shape)
        shape[axis] = width * self.planes
        joined = jnp.zeros(shape, block.dtype)
        for index, piece in found:
            joined = lax.dynamic_update_slice_in_dim(joined, piece, index * width, axis)
        return joined

    def scatter_tokens(self, block):
        tail = block.shape[1:]
        block = block.reshape((self.planes, self.split) + tail)
        block = jnp.moveaxis(block, 1, 0)
        block = self.sum_parts(block)
        group = self.group()
        half = tail[0] // 2
        colours = [block[:, :half], block[:, half:]]
        orders = [list(self.group_bits), list(reversed(self.group_bits))]
        sizes = [2] * len(self.group_bits)
        colours = [c.reshape(tuple(sizes) + (half,) + tail[1:]) for c in colours]
        live = [list(reversed(self.group_bits)) for _ in colours]
        for step in range(len(self.group_bits)):
            for c in range(2):
                bit = orders[c][step]
                place = live[c].index(bit)
                live[c].pop(place)
                halves = jnp.moveaxis(colours[c], place, 0)
                mine = (group // bit) % 2
                got = self.send(
                    pick(halves, 1 - mine).astype(bf16),
                    lambda g, u, z, bit=bit: (g ^ bit, u, z),
                )
                colours[c] = pick(halves, mine) + got.astype(f32)
        return jnp.concatenate(colours, axis=0)


FAR_CHUNK = 128
DECODE_CHUNKS = 2


def per_device(
    context,
    out_grad,
    rewards,
    master,
    first_moment,
    second_moment,
    inputs,
    w_query,
    w_key,
    w_value,
    cache_keys,
    cache_values,
    lengths,
):
    replicas = lax.axis_size("rep")
    planes = lax.axis_size("tp")
    lay = Layout(replicas, planes)
    split = lay.split
    tokens, features = context.shape
    columns = out_grad.shape[1]
    own_rows = features // split
    plane = lax.axis_index("tp")

    pair_grad = lay.send(out_grad, lambda g, u, z: (g, u, z ^ 1))
    hub_rows = {}
    for stride in lay.strides:
        hub_rows[stride] = lay.send(
            context,
            lambda g, u, z, stride=stride: (
                (g, u, lay.hub((z // 2) ^ stride)) if lay.is_hub(z) else None
            ),
        )

    width = FAR_CHUNK if own_rows % FAR_CHUNK == 0 else own_rows
    count = own_rows // width
    by_part = context.reshape(tokens, split, own_rows)
    far_rows = []
    for k in range(count):
        chunk = by_part[:, :, k * width : (k + 1) * width].reshape(tokens, split * width)
        if k == 0:
            waits = [pair_grad] + list(hub_rows.values())
        else:
            waits = far_rows[k - 1]
        tied = lax.optimization_barrier(tuple([chunk] + waits))
        chunk = tied[0]
        if k == 0:
            pair_grad = tied[1]
            hub_rows = dict(zip(lay.strides, tied[2:]))
        else:
            far_rows[k - 1] = list(tied[1:])
        far_rows.append(
            [
                lay.send(
                    chunk,
                    lambda g, u, z, stride=stride: (
                        None if lay.is_hub(z) else (g, u, lay.hub((z // 2) ^ stride))
                    ),
                )
                for stride in lay.strides
            ]
        )

    attended = decode_heads(inputs, w_query, w_key, w_value, cache_keys, cache_values, lengths)
    all_heads = lay.gather_planes(attended, 1)
    feature_rows = lax.all_to_all(all_heads, "rep", split_axis=1, concat_axis=0, tiled=True)

    scale = token_scale(context, rewards)[:, None]
    own_grad = lax.optimization_barrier((out_grad.astype(f32) * scale).astype(bf16))
    pair_grad = lax.optimization_barrier((pair_grad.astype(f32) * scale).astype(bf16))

    def product(rows, grads):
        return outer_sum(rows, grads).reshape(split, rows.shape[1] // split, columns)

    own_own = lay.sum_to_owner(
        lay.sum_parts(product(context, own_grad)), "own", lay.group_bits
    )
    own_other = lay.reduce_own_other(product(context, pair_grad))
    group = lay.group()
    early = jnp.where(group == plane, own_own.astype(bf16), own_other)
    hub_here = lay.table([lay.is_hub(z) for z in range(planes)])

    def choose(current, kind, parts):
        owner = lay.table([lay.source(lay.hub(z // 2), kind) for z in range(planes)])
        kept, came = parts
        return jnp.where(
            group == owner, jnp.where(hub_here, kept.astype(bf16), came), current
        )

    high = lay.group_bits[-1]
    low = lay.group_bits[0]
    for stride in lay.strides:
        kind = ("hub", stride)
        rows = hub_rows[stride]
        parts = lay.reduce_pair(product(rows, own_grad), product(rows, pair_grad), kind, high)
        early = choose(early, kind, parts)

    steps = []
    weights = []
    for k in range(count):
        spot = slice(k * width, (k + 1) * width)
        gradient = early[spot]
        for stride, rows in zip(lay.strides, far_rows[k]):
            kind = ("outer", stride)
            parts = lay.reduce_pair(product(rows, own_grad), product(rows, pair_grad), kind, low)
            gradient = choose(gradient, kind, parts)
        step = adam(gradient.astype(f32), first_moment[spot], second_moment[spot])
        steps.append(step)
        weights.append((master[spot] - learn_rate * step).astype(bf16))
    adam_step = jnp.concatenate(steps, axis=0)

    step_total, seq_local, model_width = inputs.shape
    local_tokens = step_total * seq_local
    last = (count - 1) * width
    pieces = []
    strip = columns // DECODE_CHUNKS
    for d in range(DECODE_CHUNKS):
        cols = slice(d * strip, (d + 1) * strip)
        partial = jnp.dot(
            feature_rows[:, last:], weights[-1][:, cols], preferred_element_type=f32
        )
        if count > 1:
            head = jnp.concatenate([w[:, cols] for w in weights[:-1]], axis=0)
            partial = partial + jnp.dot(
                feature_rows[:, :last], head, preferred_element_type=f32
            )
        own = lay.scatter_tokens(partial.reshape(replicas, local_tokens, strip))
        pieces.append(lay.gather_planes(own.astype(bf16)[:, None, :], 1))
    decoded = jnp.concatenate(pieces, axis=2)
    return (decoded.reshape(step_total, seq_local, model_width), adam_step)


def solution(mesh):
    placed = (
        P("rep", "tp"),
        P("rep", "tp"),
        P(None, "rep"),
        P("rep", "tp"),
        P("rep", "tp"),
        P("rep", "tp"),
        P(None, "rep", None),
        P(None, "tp"),
        P(None, "tp"),
        P(None, "tp"),
        P("rep", None, "tp"),
        P("rep", None, "tp"),
        P("rep"),
    )
    return jax.shard_map(
        per_device,
        mesh=mesh,
        in_specs=placed,
        out_specs=(P(None, "rep", None), P("rep", "tp")),
        check_vma=False,
    )
```

```python
import math

import jax
import jax.numpy as jnp
from jax import lax
from jax.experimental.layout import Layout as MemoryLayout, with_layout_constraint
from jax.sharding import PartitionSpec as P


HEAD_DIM = 128


rope_base = 1000000.0
first_beta = 0.9
second_beta = 0.95
adam_epsilon = 1e-08
step_count = 10
learn_rate = 0.001


bf16 = jnp.bfloat16
f32 = jnp.float32
AXES = ("rep", "tp")
ROW_MAJOR = MemoryLayout(major_to_minor=(0, 1))


def rotate(vectors, positions):
    half_dim = vectors.shape[-1] // 2
    frequency = rope_base ** (-2.0 * jnp.arange(half_dim, dtype=jnp.float32) / vectors.shape[-1])
    angles = positions[..., None].astype(jnp.float32) * frequency
    cosine_table = jnp.cos(angles)
    sine_table = jnp.sin(angles)
    former = vectors[..., :half_dim]
    latter = vectors[..., half_dim:]
    return jnp.concatenate(
        [former * cosine_table - latter * sine_table, latter * cosine_table + former * sine_table],
        axis=-1,
    )


def attend(queries, old_keys, old_values, new_keys, new_values, live_mask):
    score_scale = HEAD_DIM ** (-0.5)
    step_total = queries.shape[0]
    cache_scores = (
        jnp.einsum("tsqd,scd->tsqc", queries, old_keys, preferred_element_type=jnp.float32)
        * score_scale
    )
    cache_scores = jnp.where(live_mask[None, :, None, :], cache_scores, -1e30)
    recent = (
        jnp.einsum("tsqd,usd->tsqu", queries, new_keys, preferred_element_type=jnp.float32)
        * score_scale
    )
    causal = jnp.arange(step_total)[:, None] >= jnp.arange(step_total)[None, :]
    recent = jnp.where(causal[:, None, None, :], recent, -1e30)
    row_peak = jnp.maximum(jnp.max(cache_scores, axis=-1), jnp.max(recent, axis=-1))[..., None]
    cache_exp = jnp.exp(cache_scores - row_peak)
    recent_exp = jnp.exp(recent - row_peak)
    denominator = jnp.sum(cache_exp, axis=-1, keepdims=True) + jnp.sum(
        recent_exp, axis=-1, keepdims=True
    )
    cache_weight = (cache_exp / denominator).astype(jnp.bfloat16)
    recent_weight = (recent_exp / denominator).astype(jnp.bfloat16)
    attended = jnp.einsum(
        "tsqc,scd->tsqd", cache_weight, old_values, preferred_element_type=jnp.float32
    )
    attended = attended + jnp.einsum(
        "tsqu,usd->tsqd", recent_weight, new_values, preferred_element_type=jnp.float32
    )
    return attended.astype(jnp.bfloat16)


def decode_heads(inputs, w_query, w_key, w_value, cache_keys, cache_values, lengths):
    step_total, seq_local, model_width = inputs.shape
    local_heads = w_query.shape[1] // HEAD_DIM
    local_kv = w_key.shape[1] // HEAD_DIM
    shared = local_heads // local_kv
    flat_rows = inputs.reshape(step_total * seq_local, model_width)
    query_flat = jnp.dot(flat_rows, w_query, preferred_element_type=jnp.float32)
    key_flat, value_flat = (
        jnp.dot(flat_rows, w, preferred_element_type=jnp.float32) for w in (w_key, w_value)
    )
    query_flat, key_flat, value_flat = lax.optimization_barrier(
        (query_flat, key_flat, value_flat)
    )
    seq_length = jnp.repeat(lengths, seq_local // lengths.shape[0])
    positions = seq_length[None, :] + jnp.arange(step_total, dtype=jnp.int32)[:, None]
    slot_total = cache_keys.shape[1]
    live_mask = jnp.arange(slot_total, dtype=jnp.int32)[None, :] < seq_length[:, None]
    heads = []
    for kv in range(local_kv):
        lanes = slice(kv * HEAD_DIM, (kv + 1) * HEAD_DIM)
        wide = slice(kv * shared * HEAD_DIM, (kv + 1) * shared * HEAD_DIM)
        queries = query_flat[:, wide].reshape(step_total, seq_local, shared, HEAD_DIM)
        queries = rotate(queries, positions[:, :, None]).astype(jnp.bfloat16)
        key_new = key_flat[:, lanes].reshape(step_total, seq_local, HEAD_DIM)
        key_new = rotate(key_new, positions).astype(jnp.bfloat16)
        value_new = value_flat[:, lanes].reshape(step_total, seq_local, HEAD_DIM)
        attended = attend(
            queries,
            cache_keys[:, :, lanes],
            cache_values[:, :, lanes],
            key_new,
            value_new.astype(jnp.bfloat16),
            live_mask,
        )
        heads.append(attended.reshape(step_total * seq_local, shared * HEAD_DIM))
    return jnp.concatenate(heads, axis=1)


def token_scale(rewards, totals, token_local):
    replicas = lax.axis_size("rep")
    prompt_count, local_group = rewards.shape
    group_size = local_group * replicas
    advantage = rewards.astype(jnp.float32) - totals.astype(jnp.float32)[:, None] / group_size
    return jnp.repeat(advantage.reshape(-1), token_local // (prompt_count * local_group)) / (
        token_local * replicas
    )


def adam(gradient, first_moment, second_moment):
    moment_new = first_beta * first_moment + (1.0 - first_beta) * gradient
    square_new = second_beta * second_moment + (1.0 - second_beta) * gradient * gradient
    return (
        moment_new
        / (1.0 - first_beta**step_count)
        / (jnp.sqrt(square_new / (1.0 - second_beta**step_count)) + adam_epsilon)
    )


def outer_sum(rows, columns):
    return lax.dot_general(
        rows, columns, (((0,), (0,)), ((), ())), preferred_element_type=jnp.float32
    )


def bits_below(count):
    found = []
    bit = 1
    while bit < count:
        found.append(bit)
        bit *= 2
    return found


def pick(array, index):
    return lax.dynamic_index_in_dim(array, index, 0, keepdims=False)


class Layout:
    def __init__(self, replicas, planes):
        self.replicas = replicas
        self.planes = planes
        self.split = replicas // planes
        self.group_bits = bits_below(planes)
        self.split_bits = bits_below(self.split)
        self.strides = range(1, planes // 2)

    def hub(self, pair):
        return 2 * pair + 1 if pair < self.planes // 4 or self.planes == 2 else 2 * pair

    def outer(self, pair):
        return self.hub(pair) ^ 1

    def is_hub(self, plane):
        return self.hub(plane // 2) == plane

    def far_hub(self, plane, stride):
        return self.hub((plane // 2) ^ stride)

    def crosses(self, stride):
        return bool(stride & (self.planes // 4))

    def table(self, values):
        return pick(jnp.array(values), lax.axis_index("tp"))

    def send(self, array, target):
        moves = []
        for rep in range(self.replicas):
            for plane in range(self.planes):
                to = target(rep // self.split, rep % self.split, plane)
                if to is not None:
                    group, part, other = to
                    moves.append(
                        (
                            rep * self.planes + plane,
                            (group * self.split + part) * self.planes + other,
                        )
                    )
        return lax.ppermute(array, AXES, moves)

    def group(self):
        return lax.axis_index("rep") // self.split

    def part(self):
        return lax.axis_index("rep") % self.split

    def sum_parts(self, blocks):
        part = self.part()
        for bit in reversed(self.split_bits):
            mine = (part // bit) % 2
            halves = [b.reshape((2, bit) + b.shape[1:]) for b in blocks]
            away = jnp.stack([pick(h, 1 - mine) for h in halves]).astype(bf16)
            got = self.send(away, lambda g, u, z, bit=bit: (g, u ^ bit, z))
            blocks = [pick(h, mine) + got[k].astype(f32) for k, h in enumerate(halves)]
        return [b[0] for b in blocks]

    def scatter_groups(self, pieces, index):
        half = pieces[0].shape[0] // 2
        live = [dict(enumerate(p[:half] for p in pieces))]
        live.append(dict(enumerate(p[half:] for p in pieces)))
        orders = [list(self.group_bits), list(reversed(self.group_bits))]
        for step in range(len(self.group_bits)):
            for c in range(2):
                bit = orders[c][step]
                mine = (index // bit) % 2 == 1
                low = [k for k in sorted(live[c]) if not k & bit]
                away = [jnp.where(mine, live[c][k], live[c][k | bit]).astype(bf16) for k in low]
                got = self.send(
                    jnp.concatenate(away, axis=0), lambda g, u, z, bit=bit: (g ^ bit, u, z)
                )
                got = jnp.split(got, len(low), axis=0)
                live[c] = {
                    k: jnp.where(mine, live[c][k | bit], live[c][k]) + got[n].astype(f32)
                    for n, k in enumerate(low)
                }
        return jnp.concatenate([live[0][0], live[1][0]], axis=0)

    def gather_planes(self, block):
        plane = lax.axis_index("tp")
        found = [(plane, block)]
        partner = self.send(block, lambda g, u, z: (g, u, z ^ 1))
        hub_here = self.table([self.is_hub(z) for z in range(self.planes)])

        def out(g, u, z):
            return (g, u, z ^ 1) if self.is_hub(z) else None

        for name, source in (("hub", block), ("outer", partner)):
            for stride in self.strides:

                def hop(g, u, z, stride=stride):
                    return (g, u, self.far_hub(z, stride)) if self.is_hub(z) else None

                got = self.send(source, hop)
                passed = self.send(got, out)
                order = [self.far_hub(z, stride) for z in range(self.planes)]
                if name == "outer":
                    order = [z ^ 1 for z in order]
                found.append((self.table(order), jnp.where(hub_here, got, passed)))
            if name == "hub":
                found.insert(1, (plane ^ 1, partner))
        return found


DECODE_CHUNKS = 2


def chunk_widths(rows):
    unit = math.gcd(rows, 128)
    units = rows // unit
    if units < 3:
        return [unit] * units
    rest = units - 1
    return [unit * (rest - rest // 2), unit * (rest // 2), unit]


def per_device(
    context,
    out_grad,
    rewards,
    master,
    first_moment,
    second_moment,
    inputs,
    w_query,
    w_key,
    w_value,
    cache_keys,
    cache_values,
    lengths,
):
    replicas = lax.axis_size("rep")
    planes = lax.axis_size("tp")
    lay = Layout(replicas, planes)
    split = lay.split
    tokens, features = context.shape
    columns = out_grad.shape[1]
    own_rows = features // split
    plane = lax.axis_index("tp")

    pair_grad = lay.send(out_grad, lambda g, u, z: (g, u, z ^ 1))
    crossing = [s for s in lay.strides if lay.crosses(s)]
    hub_rows = {
        s: lay.send(
            context,
            lambda g, u, z, s=s: (g, u, lay.far_hub(z, s)) if lay.is_hub(z) else None,
        )
        for s in crossing
    }
    widths = chunk_widths(own_rows)
    spots = [slice(sum(widths[:k]), sum(widths[: k + 1])) for k in range(len(widths))]

    def chunk_of(rows, spot):
        return jnp.concatenate(
            [rows[:, u * own_rows + spot.start : u * own_rows + spot.stop] for u in range(split)],
            axis=1,
        )

    chunks = [chunk_of(context, spot) for spot in spots]

    def send_far(chunk):
        found = {}
        for s in lay.strides:
            if lay.crosses(s):
                found[s] = lay.send(
                    chunk,
                    lambda g, u, z, s=s: None if lay.is_hub(z) else (g, u, lay.far_hub(z, s)),
                )
            else:
                found[s] = lay.send(chunk, lambda g, u, z, s=s: (g, u, z ^ (2 * s)))
        return found

    totals = lax.psum(jnp.sum(rewards, axis=1), "rep")
    inputs, totals = lax.optimization_barrier((inputs, totals))
    scale = token_scale(rewards, totals, tokens)[:, None]
    own_grad = lax.optimization_barrier((out_grad.astype(f32) * scale).astype(bf16))

    attended = decode_heads(inputs, w_query, w_key, w_value, cache_keys, cache_values, lengths)
    pieces = lay.gather_planes(attended)
    partner, *chunks = lax.optimization_barrier((pieces[1][1], *chunks))
    pieces[1] = (pieces[1][0], partner)
    all_heads = jnp.zeros((attended.shape[0], features * planes), bf16)
    for index, piece in pieces:
        all_heads = lax.dynamic_update_slice_in_dim(all_heads, piece, index * features, 1)
    far_rows = []
    for k, chunk in enumerate(chunks):
        if k > 1:
            names = list(far_rows[k - 2])
            chunk, *before = lax.optimization_barrier((chunk, *far_rows[k - 2].values()))
            far_rows[k - 2] = dict(zip(names, before))
        far_rows.append(send_far(chunk))
    feature_rows = lax.all_to_all(all_heads, "rep", split_axis=1, concat_axis=0, tiled=True)
    feature_rows = with_layout_constraint(feature_rows, ROW_MAJOR)

    def product(rows, grads):
        return outer_sum(rows, grads).reshape(split, rows.shape[1] // split, columns)

    own_own = product(context, own_grad)
    own_own, pair_grad = lax.optimization_barrier((own_own, pair_grad))
    pair_grad = lax.optimization_barrier((pair_grad.astype(f32) * scale).astype(bf16))
    hub_here = lay.table([lay.is_hub(z) for z in range(planes)])
    passed = []
    for k, spot in enumerate(spots):
        onward = {s: chunk_of(hub_rows[s], spot) for s in crossing}
        if k > 1 and crossing:
            tied = lax.optimization_barrier((onward, passed[k - 2]))
            onward, passed[k - 2] = tied
        passed.append(
            {
                s: lay.send(
                    onward[s], lambda g, u, z: (g, u, z ^ 1) if lay.is_hub(z) else None
                )
                for s in crossing
            }
        )
    own_other = product(context, pair_grad)
    own_sums = lay.sum_parts([own_own, own_other])

    relative = lay.group() ^ plane
    odd = relative % 2 == 1

    def swap(g, u, z):
        return (g ^ 1, u, z ^ 1) if (g ^ z) & 1 else None

    steps = []
    weights = []
    for k, spot in enumerate(spots):
        parts = []
        for s in lay.strides:
            rows = far_rows[k][s]
            if s in passed[k]:
                rows = lax.optimization_barrier(jnp.where(hub_here, rows, passed[k][s]))
            parts += [product(rows, own_grad), product(rows, pair_grad)]
        sums = [block[spot] for block in own_sums]
        if parts:
            sums += lay.sum_parts(parts)
        kept = lay.scatter_groups(sums, relative).astype(bf16)
        gradient = jnp.where(odd, lay.send(kept, swap), kept)
        step = adam(gradient.astype(f32), first_moment[spot], second_moment[spot])
        steps.append(step)
        weights.append((master[spot] - learn_rate * step).astype(bf16))

    step_total, seq_local, model_width = inputs.shape
    local_tokens = step_total * seq_local
    decoded = jnp.zeros((local_tokens, model_width), bf16)
    strip = columns // DECODE_CHUNKS
    for d in range(DECODE_CHUNKS):
        cols = slice(d * strip, (d + 1) * strip)
        partial = 0.0
        if len(weights) > 1:
            head = jnp.concatenate([w[:, cols] for w in weights[:-1]], axis=0)
            partial = jnp.dot(
                feature_rows[:, : spots[-1].start], head, preferred_element_type=f32
            )
            partial = lax.optimization_barrier(partial)
        partial = partial + jnp.dot(
            feature_rows[:, spots[-1]], weights[-1][:, cols], preferred_element_type=f32
        )
        partial = with_layout_constraint(partial, ROW_MAJOR)
        by_part = partial.reshape(planes, split, local_tokens, strip)
        by_part = lay.sum_parts([jnp.moveaxis(by_part, 1, 0)])[0]
        own = lay.scatter_groups([by_part[g] for g in range(planes)], lay.group()).astype(bf16)
        if d == DECODE_CHUNKS - 1:
            own, *steps = lax.optimization_barrier((own, *steps))
        for index, piece in lay.gather_planes(own):
            decoded = lax.dynamic_update_slice(
                decoded, piece, (0, index * columns + d * strip)
            )
    adam_step = jnp.concatenate(steps, axis=0)
    return (decoded.reshape(step_total, seq_local, model_width), adam_step)


def solution(mesh):
    placed = (
        P("rep", "tp"),
        P("rep", "tp"),
        P(None, "rep"),
        P("rep", "tp"),
        P("rep", "tp"),
        P("rep", "tp"),
        P(None, "rep", None),
        P(None, "tp"),
        P(None, "tp"),
        P(None, "tp"),
        P("rep", None, "tp"),
        P("rep", None, "tp"),
        P("rep"),
    )

    return jax.shard_map(
        per_device,
        mesh=mesh,
        in_specs=placed,
        out_specs=(P(None, "rep", None), P("rep", "tp")),
        check_vma=False,
    )
```
